128 devices in a mesh: replica: 4 (over z), shard: 16 (over y, x_lo, core), tensor: 2 (over x_hi).
Axes of the slice: x: 4 (x_hi: 2, x_lo: 2; x = x_hi * 2 + x_lo), y: 4, z: 4, core: 2. Of those that a mesh axis runs over, the one named last changes fastest.
Arguments:
- trained_up: bfloat16 [4, 1024, 4096], P('replica', None, 'tensor'), may hold values from -6 to 6
- trained_down: bfloat16 [4, 4096, 1024], P('replica', 'tensor'), may hold values from -6 to 6
- trained_embed: bfloat16 [4, 32768, 1024], P('replica', ('shard', 'tensor')), may hold values from -6 to 6
- trained_norm: bfloat16 [4, 2, 1024], P('replica'), may hold values from 0.099609375 to 1.8984375
- master_up: float32 [1024, 4096], P(('replica', 'shard', 'tensor')), may hold values from -6 to 6
- moment_up: float32 [1024, 4096], P(('replica', 'shard', 'tensor')), may hold values from -4 to 4
- master_down: float32 [2, 2048, 1024], P('tensor', ('replica', 'shard')), may hold values from -6 to 6
- moment_down: float32 [2, 2048, 1024], P('tensor', ('replica', 'shard')), may hold values from -4 to 4
- master_embed: float32 [32, 1024, 1024], P(('shard', 'tensor'), 'replica'), may hold values from -6 to 6
- moment_embed: float32 [32, 1024, 64], P(('shard', 'tensor'), 'replica'), may hold values from -4 to 4
- master_norm: float32 [2, 1024], replicated, may hold values from 0.1 to 1.9
- moment_norm: float32 [2, 1024], replicated, may hold values from -2 to 2
- embed_basis: float32 [1024, 64], replicated, may hold values from -0.1875 to 0.1875
Outputs:
- recast_up: bfloat16 [1024, 4096], P(None, 'tensor')
- recast_down: bfloat16 [4096, 1024], P('tensor')
- recast_embed: bfloat16 [32768, 1024], P(('shard', 'tensor'))
- recast_norm: bfloat16 [2, 1024], replicated
- stored_up: float32 [1024, 4096], P(('replica', 'shard', 'tensor'))
- velocity_up: float32 [1024, 4096], P(('replica', 'shard', 'tensor'))
- stored_down: float32 [2, 2048, 1024], P('tensor', ('replica', 'shard'))
- velocity_down: float32 [2, 2048, 1024], P('tensor', ('replica', 'shard'))
- stored_embed: float32 [32, 1024, 1024], P(('shard', 'tensor'), 'replica')
- velocity_embed: float32 [32, 1024, 64], P(('shard', 'tensor'), 'replica')
- stored_norm: float32 [2, 1024], replicated
- velocity_norm: float32 [2, 1024], replicated
The draws below stay inside these ranges and needn't reach their ends.
All inputs are finite; a program needn't handle non-finite values.
Results may differ from the reference program's by a relative error of at most 0.012.
Values may be sent and summed in bfloat16 or wider, within the bound.
A program may use at most 128 MiB of HBM per device.

```python
import jax
import jax.numpy as jnp
from jax import lax

D = 1024
FF = 4096
RANK = 64
EMB_DEV = 256
EMB_ROWS = 32768
N_REPLICA = 4
N_SHARD = 16
N_TENSOR = 2


def shard_levels(rng, dims, split, smallest, top_value):
    factor_of, own = 1.0, jax.random.fold_in(rng, 6)
    for dim, shards_of in split:
        heights = jnp.exp(jax.random.uniform(jax.random.fold_in(own, dim), (shards_of,), jnp.float32, smallest / len(split), top_value / len(split)))
        factor_of = factor_of * jnp.repeat(heights, dims[dim] // shards_of).reshape([-1 if axis == dim else 1 for axis in range(len(dims))])
    return factor_of


def noise(stream_key, dims, spread, limit, cuts=(), dtype=jnp.bfloat16):
    values = jax.random.normal(stream_key, dims, jnp.float32) * spread
    if len(cuts) > 0:
        values = shard_levels(stream_key, dims, cuts, -0.22, 0.18) * values
    return jnp.clip(values, min=-limit, max=limit).astype(dtype)


def setup_inputs(seed: int = 0) -> dict:
    keys = jax.random.split(jax.random.key(seed), 14)
    return {
        "trained_up": noise(keys[0], (N_REPLICA, D, FF), 1.0, 6.0, ((0, 4), (2, 2))),
        "trained_down": noise(keys[1], (N_REPLICA, FF, D), 1.0, 6.0, ((0, 4), (1, 2))),
        "trained_embed": noise(keys[2], (N_REPLICA, EMB_ROWS, D), 1.0, 6.0, ((0, 4), (1, 32))),
        "trained_norm": jnp.clip(1.0 + 0.18 * jax.random.normal(keys[3], (N_REPLICA, 2, D), jnp.float32), 0.099609375, 1.8984375).astype(jnp.bfloat16),
        "master_up": noise(keys[4], (D, FF), 1.0, 6.0, ((0, 128),), jnp.float32),
        "moment_up": noise(keys[5], (D, FF), 0.5, 4.0, ((0, 128),), jnp.float32),
        "master_down": noise(keys[6], (N_TENSOR, FF // N_TENSOR, D), 1.0, 6.0, ((0, 2), (1, 64)), jnp.float32),
        "moment_down": noise(keys[7], (N_TENSOR, FF // N_TENSOR, D), 0.5, 4.0, ((0, 2), (1, 64)), jnp.float32),
        "master_embed": noise(keys[8], (N_SHARD * N_TENSOR, N_REPLICA * EMB_DEV, D), 1.0, 6.0, ((0, 32), (1, 4)), jnp.float32),
        "moment_embed": noise(keys[9], (N_SHARD * N_TENSOR, N_REPLICA * EMB_DEV, RANK), 0.5, 4.0, ((0, 32), (1, 4)), jnp.float32),
        "master_norm": jnp.clip(1.0 + 0.18 * jax.random.normal(keys[10], (2, D), jnp.float32), 0.1, 1.9),
        "moment_norm": noise(keys[11], (2, D), 0.2, 2.0, (), jnp.float32),
        "embed_basis": noise(keys[12], (D, RANK), D ** -0.5, 0.1875, (), jnp.float32),
    }


def outer_step(master, moment, summed, groups):
    difference = master - summed / groups
    velocity = 0.5 * moment + difference
    return master - 0.7 * (difference + 0.5 * velocity), velocity


def reference(trained_up, trained_down, trained_embed, trained_norm, master_up, moment_up, master_down, moment_down, master_embed, moment_embed, master_norm, moment_norm, embed_basis):
    up_total = jnp.sum(trained_up.astype(jnp.float32), axis=0)
    stored_up, velocity_up = outer_step(master_up, moment_up, up_total, N_REPLICA)
    down_total = jnp.sum(trained_down.astype(jnp.float32), axis=0).reshape(N_TENSOR, FF // N_TENSOR, D)
    stored_down, velocity_down = outer_step(master_down, moment_down, down_total, N_REPLICA)
    norm_total = jnp.sum(trained_norm.astype(jnp.float32), axis=0)
    stored_norm, velocity_norm = outer_step(master_norm, moment_norm, norm_total, N_REPLICA)
    embed_total = jnp.zeros((EMB_ROWS, D), jnp.float32)
    for group in range(N_REPLICA):
        embed_total = embed_total + trained_embed[group].astype(jnp.float32)
    flat_master = master_embed.reshape(EMB_ROWS, D)
    coefficient = jnp.dot(flat_master - embed_total / N_REPLICA, embed_basis, precision=lax.Precision.HIGHEST)
    velocity_flat = 0.5 * moment_embed.reshape(EMB_ROWS, RANK) + coefficient
    stored_flat = flat_master - 0.7 * jnp.dot(coefficient + 0.5 * velocity_flat, embed_basis.T, precision=lax.Precision.HIGHEST)
    return (stored_up.astype(jnp.bfloat16), stored_down.reshape(FF, D).astype(jnp.bfloat16), stored_flat.astype(jnp.bfloat16), stored_norm.astype(jnp.bfloat16), stored_up, velocity_up, stored_down, velocity_down, stored_flat.reshape(master_embed.shape), velocity_flat.reshape(moment_embed.shape), stored_norm, velocity_norm)
```

```python
import jax
import jax.numpy as jnp
from jax import lax
from jax.experimental import pallas as pl
from jax.experimental.pallas import tpu as pltpu
from jax.sharding import PartitionSpec as P

MESH = pl.DeviceIdType.MESH
F32, BF16 = jnp.float32, jnp.bfloat16

ORDER = [
    "D030", "D010", "D001", "D300", "D100", "U001", "U030", "U010", "U300", "U100",
    "m1", "pw",
    "D020", "D031", "D310", "D011", "D330", "D110", "D200", "D301", "D130", "r0",
    "U011", "D101", "U031", "U310", "U020", "D021", "U110", "U301", "U101",
    "m2", "m3", "U330", "D311", "U200", "D320", "x", "U130", "D331", "D120", "D111", "D230", "D210",
    "D201", "U331", "U021", "r1", "D131", "U131", "U201", "e0", "U320", "U230", "D321", "U120", "D121", "D220",
    "U311", "D231", "e1", "U321", "U111", "D211", "U121", "U210", "U220", "D221", "U211", "U231", "U221",
]


def routes(kind, o, p, e):
    every_y = [("y+", ""), ("y-", "")]
    if kind == "D":
        if p == 0 and e == 0:
            z_part = {0: [("z+", ""), ("z-", "")], 3: [("z+", "a")], 1: [("z-", "b")], 2: []}[o]
            return z_part + every_y + [("x", ""), ("c", "")]
        if e == 0:
            relay = [("y+", "")] if p == 3 and o % 2 == 0 else [("y-", "")] if p == 1 and o % 2 == 1 else []
            return relay + [("x", ""), ("c", "")]
        return [("c", "")]
    if p == 0:
        x_part = [("x", "")] if o == 0 and e == 0 else []
        z_part = {0: [("z+", ""), ("z-", "")], 3: [("z+", "a")], 1: [("z-", "b")], 2: []}[o]
        return x_part + z_part + every_y + [("c", "")]
    odd = (o + e) % 2
    relay = [("y+", "")] if p == 3 and not odd else [("y-", "")] if p == 1 and odd else []
    return relay + [("c", "")]


def seen_from(direction, o, p, e):
    if direction == "z+":
        return (o + 3) % 4, p, e
    if direction == "z-":
        return (o + 1) % 4, p, e
    if direction == "y+":
        return o, (p + 3) % 4, e
    if direction == "y-":
        return o, (p + 1) % 4, e
    if direction == "x":
        return o, p, 1 - e
    return o, p, e


def outer_step(master, moment, summed):
    difference = master - summed * 0.25
    velocity = 0.5 * moment + difference
    return master - 0.7 * (difference + 0.5 * velocity), velocity


def nt_dot(a, b):
    return lax.dot_general(a, b, (((1,), (1,)), ((), ())), preferred_element_type=F32)


SLOTS = {}


def slot(key):
    return SLOTS.setdefault(key, len(SLOTS))


N_RECV = 104
N_SEND = 56


def exchange(
    tu, td, te, tn, mu, vu, md, vd, me, ve, mn, vn, bt,
    RU, RD, RE, RN, SU, VU, SD, VD, SE, VE, SN, VN,
    tu_v, td_v, te_v, nb, mu_v, vu_v, md_v, vd_v, m_v, ve_v, mn_v, vn_v, bt_v,
    ru_a, ru_m, ru_p, rd_a, rd_m, rd_p, su, sd, cs, cr, xs, xr, so,
    bs, mb, pf, pp, pr, wv, ms,
    lsem, ssem, gsem, rsem, csem,
):
    SLOTS.clear()
    z, s, t = lax.axis_index("replica"), lax.axis_index("shard"), lax.axis_index("tensor")
    y, x, c = lax.div(s, 4), lax.rem(lax.div(s, 2), 2), lax.rem(s, 2)
    zo = [z] + [lax.rem(z + i, 4) for i in (1, 2, 3)]
    yo = [y] + [lax.rem(y + i, 4) for i in (1, 2, 3)]
    xo = [x, 1 - x]
    devices = {
        "z+": (zo[1], s, t),
        "z-": (zo[3], s, t),
        "z2": (zo[2], s, t),
        "y+": (z, yo[1] * 4 + x * 2 + c, t),
        "y-": (z, yo[3] * 4 + x * 2 + c, t),
        "x": (z, y * 4 + xo[1] * 2 + c, t),
        "c": (z, y * 4 + x * 2 + (1 - c), t),
        "t": (z, s, 1 - t),
    }

    def block(o, p, e, core=c):
        return zo[o] * 16 + yo[p] * 4 + xo[e] * 2 + core

    loads = {}

    def load(name, src, dst):
        loads[name] = pltpu.make_async_copy(src, dst, lsem.at[len(loads)])
        loads[name].start()

    load("tu", tu.at[:, s], tu_v)
    load("td", td.at[:, s], td_v)
    load("mu", mu, mu_v)
    load("vu", vu, vu_v)
    load("md", md, md_v)
    load("vd", vd, vd_v)
    load("tn", tn, nb.at[z])
    load("me", me, m_v)
    load("bt", bt, bt_v)
    load("te", te, te_v)
    load("ve", ve, ve_v)
    load("mn", mn, mn_v)
    load("vn", vn, vn_v)

    barrier = pltpu.get_barrier_semaphore()
    for device in devices.values():
        pl.semaphore_signal(barrier, inc=1, device_id=device, device_id_type=MESH)
    pl.semaphore_wait(barrier, len(devices))

    single = []
    grouped = {}
    group_index = {"z+": 0, "z-": 1, "y+": 2, "y-": 3, "x": 4, "c": 5}

    def push(src, dst, key, direction):
        copy = pltpu.make_async_remote_copy(
            src, dst, ssem.at[len(single)], rsem.at[slot(key)], device_id=devices[direction], device_id_type=MESH
        )
        copy.start()
        single.append(copy)

    def arrived(ref, key):
        pltpu.make_async_remote_copy(
            ref, ref, ssem.at[0], rsem.at[slot(key)], device_id=devices["c"], device_id_type=MESH
        ).wait_recv()

    gathered = {"D": RD, "U": RU}
    half_rows = {"D": 16, "U": 8}

    def half_of(kind, which, index):
        n = half_rows[kind]
        return gathered[kind].at[index, pl.ds(0 if which == "a" else n, n)]

    def forward(kind, o, p, e):
        index = block(o, p, e)
        for direction, half in routes(kind, o, p, e):
            if half:
                view = half_of(kind, half, index)
                push(view, view, (kind, seen_from(direction, o, p, e), half), direction)
                continue
            view = gathered[kind].at[index]
            if direction == "c":
                recv = csem.at[0 if kind == "D" else 1]
            else:
                recv = rsem.at[slot((kind, seen_from(direction, o, p, e)))]
            pltpu.make_async_remote_copy(
                view, view, gsem.at[group_index[direction]], recv, device_id=devices[direction], device_id_type=MESH
            ).start()
            grouped[direction] = grouped.get(direction, 0) + 1

    def take(kind, o, p, e):
        index = block(o, p, e)
        if p == 0 and o == 2 and (e == 0 or kind == "U"):
            for half in "ab":
                arrived(half_of(kind, half, index), (kind, (o, p, e), half))
        else:
            arrived(gathered[kind].at[index], (kind, (o, p, e)))
        forward(kind, o, p, e)

    loads["tu"].wait()
    loads["td"].wait()
    push(tu_v.at[zo[2]], ru_a, "ru_a", "z+")
    push(td_v.at[zo[2]], rd_a, "rd_a", "z-")
    push(td_v.at[zo[1]], rd_m, "rd_m", "z+")
    push(tu_v.at[zo[3]], ru_p, "ru_p", "z-")

    on_low = t == 0

    def pick(low, high):
        return jnp.where(on_low, low, high)

    half = mu_v.shape[1] // 2
    loads["mu"].wait()
    loads["vu"].wait()
    m_other = pick(mu_v[:, half:], mu_v[:, :half])
    v_other = pick(vu_v[:, half:], vu_v[:, :half])
    cs[...] = (-0.05 * m_other - 0.175 * v_other).astype(BF16)
    push(cs, cr, "cr", "t")
    loads["tn"].wait()
    for direction, name in (("z+", "n3"), ("z-", "n1"), ("z2", "n2")):
        push(nb.at[z], nb.at[z], name, direction)

    loads["me"].wait()

    @pl.loop(0, 4)
    def _(k):
        mb[z * 4 + k] = m_v[k].astype(BF16)

    def send_master(up, down):
        push(mb.at[z * 4 + up], mb.at[z * 4 + up], ("m-", up), "z+")
        push(mb.at[z * 4 + down], mb.at[z * 4 + down], ("m+", down), "z-")

    def relay_master(up, down):
        from_minus, from_plus = mb.at[zo[3] * 4 + up], mb.at[zo[1] * 4 + down]
        arrived(from_minus, ("m-", up))
        push(from_minus, from_minus, ("m2", up), "z+")
        arrived(from_plus, ("m+", down))
        push(from_plus, from_plus, ("m2", down), "z-")

    arrived(ru_a, "ru_a")
    su[...] = (ru_a[...].astype(F32) + tu_v[zo[1]].astype(F32)).astype(BF16)
    push(su, ru_m, "ru_m", "z+")
    arrived(rd_a, "rd_a")
    sd[...] = (rd_a[...].astype(F32) + td_v[zo[3]].astype(F32)).astype(BF16)
    push(sd, rd_p, "rd_p", "z-")
    send_master(0, 2)

    loads["bt"].wait()
    high = bt_v[...].astype(BF16)
    bs[:64] = high
    bs[64:] = (bt_v[...] - high.astype(F32)).astype(BF16)
    loads["te"].wait()

    @pl.loop(0, 4)
    def _(j):
        both = nt_dot(bs[...], te_v[j])
        one = both[:64] + both[64:]
        pf[j] = one
        pp[j] = one.astype(BF16)

    for direction, o, name in (("z+", 1, "p3"), ("z-", 3, "p1"), ("z2", 2, "p2")):
        push(pp.at[zo[o]], pr.at[z], name, direction)

    loads["md"].wait()
    loads["vd"].wait()
    arrived(rd_m, "rd_m")
    arrived(rd_p, "rd_p")
    down_sum = rd_p[...].astype(F32) + rd_m[...].astype(F32) + td_v[z].astype(F32)
    stored, velocity = outer_step(md_v[...], vd_v[...], down_sum)
    RD[block(0, 0, 0)] = stored.astype(BF16)
    forward("D", 0, 0, 0)
    SD[...] = stored
    VD[...] = velocity

    arrived(ru_p, "ru_p")
    arrived(ru_m, "ru_m")
    arrived(cr, "cr")
    up_sum = ru_m[...].astype(F32) + ru_p[...].astype(F32) + tu_v[z].astype(F32)
    own, other = pick(up_sum[:8], up_sum[8:]), pick(up_sum[8:], up_sum[:8])
    m_own = pick(mu_v[:, :half], mu_v[:, half:])
    v_own = pick(vu_v[:, :half], vu_v[:, half:])
    own_new = outer_step(m_own, v_own, own)[0]
    other_new = 0.2625 * other + cr[...].astype(F32)
    RU[block(0, 0, 0)] = jnp.concatenate([pick(own_new, other_new), pick(other_new, own_new)], axis=0).astype(BF16)
    forward("U", 0, 0, 0)
    so[...] = own
    xs[...] = other.astype(BF16)
    push(xs, xr, "xr", "t")

    mq = jnp.zeros((64, 256), F32)
    loads["ve"].wait()
    for k in range(4):
        rows = m_v[k]
        low = (rows - rows.astype(BF16).astype(F32)).astype(BF16)
        both = nt_dot(bs[...], mb[z * 4 + k])
        ms[k] = both[:64] + both[64:] + nt_dot(bs[:64], low)

    def recast(o):
        w = wv[zo[o]].astype(F32).T

        for k in range(4):
            part = jnp.dot(w[k * 64 : (k + 1) * 64].astype(BF16), bs[:64], preferred_element_type=F32)
            if o == 0:
                new = m_v[k] - 0.7 * part
                SE[pl.ds(k * 64, 64)] = new
            else:
                new = mb[zo[o] * 4 + k].astype(F32) - 0.7 * part
            RE[zo[o] * 4 + k] = new.astype(BF16)

    def weights():
        for o in (1, 2, 3):
            arrived(pr.at[zo[o]], f"p{o}")
        total = pf[z] + pr[zo[1]].astype(F32) + pr[zo[2]].astype(F32) + pr[zo[3]].astype(F32)
        coefficient = jnp.concatenate([ms[k] for k in range(4)], axis=1) - 0.25 * total
        new = 0.5 * ve_v[...] + coefficient
        VE[...] = new
        wv[z] = (coefficient + 0.5 * new).astype(BF16)
        for direction, name in (("z+", "w3"), ("z-", "w1"), ("z2", "w2")):
            push(wv.at[z], wv.at[z], name, direction)
        recast(0)

    def local_steps():
        arrived(xr, "xr")
        for h in range(2):
            columns = pl.ds(h * half, half)
            mine = jnp.where(t == h, so[...], xr[...].astype(F32))
            stored, velocity = outer_step(mu_v[:, columns], vu_v[:, columns], mine)
            SU[:, columns] = stored
            VU[:, columns] = velocity
        for o in (1, 2, 3):
            arrived(nb.at[zo[o]], f"n{o}")
        loads["mn"].wait()
        loads["vn"].wait()
        total = nb[0].astype(F32) + nb[1].astype(F32) + nb[2].astype(F32) + nb[3].astype(F32)
        stored, velocity = outer_step(mn_v[...], vn_v[...], total)
        SN[...] = stored
        VN[...] = velocity
        RN[...] = stored.astype(BF16)

    def near_rows():
        for o, side in ((3, "m-"), (1, "m+")):
            for k in {"m-": (2, 3), "m+": (0, 1)}[side]:
                arrived(mb.at[zo[o] * 4 + k], (side, k))
            arrived(wv.at[zo[o]], f"w{o}")
            recast(o)

    def far_rows():
        for k in range(4):
            arrived(mb.at[zo[2] * 4 + k], ("m2", k))
        arrived(wv.at[zo[2]], "w2")
        recast(2)

    extra = {
        "m1": lambda: send_master(1, 3),
        "m2": lambda: send_master(2, 0),
        "m3": lambda: send_master(3, 1),
        "r0": lambda: relay_master(0, 2),
        "r1": lambda: relay_master(1, 3),
        "pw": weights,
        "x": local_steps,
        "e0": near_rows,
        "e1": far_rows,
    }
    for name in ORDER:
        if name in extra:
            extra[name]()
        else:
            take(name[0], int(name[1]), int(name[2]), int(name[3]))

    for i, ref in enumerate((RD, RU)):
        view = ref.at[pl.ds(0, 32)]
        pltpu.make_async_remote_copy(
            view, view, ssem.at[0], csem.at[i], device_id=devices["c"], device_id_type=MESH
        ).wait_recv()
    for copy in single:
        copy.wait_send()
    for direction, n in grouped.items():
        view = RD.at[pl.ds(0, n)]
        pltpu.make_async_remote_copy(
            view, view, gsem.at[group_index[direction]], rsem.at[0], device_id=devices["c"], device_id_type=MESH
        ).wait_send()


def flush(*refs):
    sources, targets, sem = refs[:12], refs[12:24], refs[24]
    copies = []
    for source, target in zip(sources, targets):
        pieces = 4 if source.shape[0] in (64, 16) and len(source.shape) == 3 else 1
        rows = source.shape[0] // pieces
        for i in range(pieces):
            part = pl.ds(i * rows, rows)
            copies.append(pltpu.make_async_copy(source.at[part], target.at[part], sem.at[len(copies)]))
            copies[-1].start()
    for copy in copies:
        copy.wait()


def body(
    trained_up,
    trained_down,
    trained_embed,
    trained_norm,
    master_up,
    moment_up,
    master_down,
    moment_down,
    master_embed,
    moment_embed,
    master_norm,
    moment_norm,
    embed_basis,
):
    operands = (
        trained_up.reshape(4, 16, 16, 2048),
        trained_down.reshape(4, 16, 32, 1024),
        trained_embed.reshape(4, 256, 1024),
        trained_norm[0],
        master_up,
        moment_up,
        master_down[0],
        moment_down[0],
        master_embed.reshape(4, 64, 1024),
        moment_embed[0].T,
        master_norm,
        moment_norm,
        embed_basis.T,
    )
    shapes = (
        ((64, 16, 2048), BF16),
        ((64, 32, 1024), BF16),
        ((16, 64, 1024), BF16),
        ((2, 1024), BF16),
        ((8, 4096), F32),
        ((8, 4096), F32),
        ((32, 1024), F32),
        ((32, 1024), F32),
        ((256, 1024), F32),
        ((64, 256), F32),
        ((2, 1024), F32),
        ((2, 1024), F32),
    )
    hbm = pl.BlockSpec(memory_space=pltpu.HBM)
    vmem = pl.BlockSpec(memory_space=pltpu.VMEM)
    new = pl.pallas_call(
        exchange,
        out_shape=tuple(pltpu.VMEM(shape, dtype) for shape, dtype in shapes),
        in_specs=[hbm] * 13,
        out_specs=[vmem] * 12,
        scratch_shapes=[
            pltpu.VMEM((4, 16, 2048), BF16),
            pltpu.VMEM((4, 32, 1024), BF16),
            pltpu.VMEM((4, 256, 1024), BF16),
            pltpu.VMEM((4, 2, 1024), BF16),
            pltpu.VMEM((8, 4096), F32),
            pltpu.VMEM((8, 4096), F32),
            pltpu.VMEM((32, 1024), F32),
            pltpu.VMEM((32, 1024), F32),
            pltpu.VMEM((4, 64, 1024), F32),
            pltpu.VMEM((64, 256), F32),
            pltpu.VMEM((2, 1024), F32),
            pltpu.VMEM((2, 1024), F32),
            pltpu.VMEM((64, 1024), F32),
            pltpu.VMEM((16, 2048), BF16),
            pltpu.VMEM((16, 2048), BF16),
            pltpu.VMEM((16, 2048), BF16),
            pltpu.VMEM((32, 1024), BF16),
            pltpu.VMEM((32, 1024), BF16),
            pltpu.VMEM((32, 1024), BF16),
            pltpu.VMEM((16, 2048), BF16),
            pltpu.VMEM((32, 1024), BF16),
            pltpu.VMEM((8, 2048), BF16),
            pltpu.VMEM((8, 2048), BF16),
            pltpu.VMEM((8, 2048), BF16),
            pltpu.VMEM((8, 2048), BF16),
            pltpu.VMEM((8, 2048), F32),
            pltpu.VMEM((128, 1024), BF16),
            pltpu.VMEM((16, 64, 1024), BF16),
            pltpu.VMEM((4, 64, 256), F32),
            pltpu.VMEM((4, 64, 256), BF16),
            pltpu.VMEM((4, 64, 256), BF16),
            pltpu.VMEM((4, 64, 256), BF16),
            pltpu.VMEM((4, 64, 64), F32),
            pltpu.SemaphoreType.DMA((13,)),
            pltpu.SemaphoreType.DMA((N_SEND,)),
            pltpu.SemaphoreType.DMA((6,)),
            pltpu.SemaphoreType.DMA((N_RECV,)),
            pltpu.SemaphoreType.DMA((2,)),
        ],
        compiler_params=pltpu.CompilerParams(
            collective_id=0, has_side_effects=True, vmem_limit_bytes=24 << 20
        ),
        name="exchange",
    )(*[pltpu.with_memory_space_constraint(a, pltpu.HBM) for a in operands])
    new = [pltpu.with_memory_space_constraint(a, pltpu.VMEM) for a in new]
    out = pl.pallas_call(
        flush,
        out_shape=tuple(jax.ShapeDtypeStruct(shape, dtype) for shape, dtype in shapes),
        in_specs=[vmem] * 12,
        out_specs=[hbm] * 12,
        scratch_shapes=[pltpu.SemaphoreType.DMA((21,))],
        compiler_params=pltpu.CompilerParams(vmem_limit_bytes=1 << 20),
        name="flush",
    )(*new)
    return (
        out[0].reshape(1024, 2048),
        out[1].reshape(2048, 1024),
        out[2].reshape(1024, 1024),
        out[3],
        out[4],
        out[5],
        out[6][None],
        out[7][None],
        out[8][None],
        out[9].T[None],
        out[10],
        out[11],
    )


def solution(mesh):
    in_specs = (
        P("replica", None, "tensor"),
        P("replica", "tensor", None),
        P("replica", ("shard", "tensor"), None),
        P("replica", None, None),
        P(("replica", "shard", "tensor"), None),
        P(("replica", "shard", "tensor"), None),
        P("tensor", ("replica", "shard"), None),
        P("tensor", ("replica", "shard"), None),
        P(("shard", "tensor"), "replica", None),
        P(("shard", "tensor"), "replica", None),
        P(),
        P(),
        P(),
    )
    out_specs = (
        P(None, "tensor"),
        P("tensor", None),
        P(("shard", "tensor"), None),
        P(),
        P(("replica", "shard", "tensor"), None),
        P(("replica", "shard", "tensor"), None),
        P("tensor", ("replica", "shard"), None),
        P("tensor", ("replica", "shard"), None),
        P(("shard", "tensor"), "replica", None),
        P(("shard", "tensor"), "replica", None),
        P(),
        P(),
    )
    return jax.shard_map(body, mesh=mesh, in_specs=in_specs, out_specs=out_specs, check_vma=False)
```

```python
import heapq

import jax
import jax.numpy as jnp
from jax import lax
from jax.experimental import pallas as pl
from jax.experimental.pallas import tpu as pltpu
from jax.sharding import PartitionSpec as P

MESH = pl.DeviceIdType.MESH
F32, BF16 = jnp.float32, jnp.bfloat16

OWN = (0, 0, 0)


def routes(kind, h, o, p, e):
    z_part = {0: ["z+", "z-"], 3: ["z+"] * (h == 0), 1: ["z-"] * (h == 1), 2: []}[o]
    y_part = {0: ["y+", "y-"], 3: ["y+"] * (h == 0), 1: ["y-"] * (h == 1), 2: []}[p]
    if kind == "D":
        if e:
            return []
        return (z_part if p == 0 else []) + y_part + ["x"]
    if p:
        return y_part
    return (["x"] if o == 0 and e == 0 else []) + z_part + y_part


def seen_from(direction, o, p, e):
    if direction == "z+":
        return (o + 3) % 4, p, e
    if direction == "z-":
        return (o + 1) % 4, p, e
    if direction == "y+":
        return o, (p + 3) % 4, e
    if direction == "y-":
        return o, (p + 1) % 4, e
    return o, p, 1 - e


def rank(piece, direction):
    kind, h, o, p, e = piece
    if kind == "D":
        return 1 if direction == "x" else 0
    if direction[0] == "y":
        return 2 if p == 0 else 3
    return 0 if direction == "x" else 1


FIRST = 1
NEAR, FAR = 24.4, 19.0
HOP, PIECE, LEAD = 2.2, 0.705, 2.1
READY = {("D", 0): 0.0, ("D", 1): 0.5, ("U", 0): 0.8, ("U", 1): 1.2}
EXTRA = [(12.0, "weights"), (9.0, "swap"), (17.0, "local"), (NEAR, "near"), (FAR, "far")]


def plan():
    links = ["z+", "z-", "y+", "y-", "x"]
    free = dict.fromkeys(links, 0.0)
    waiting = {link: [] for link in links}
    events, steps = [], []

    def at(when, what):
        at.count += 1
        heapq.heappush(events, (when, at.count, what))

    def offer(link, order, what):
        at.count += 1
        heapq.heappush(waiting[link], (order, at.count, what))

    at.count = 0
    for (kind, h), when in READY.items():
        at(when, ("take", (kind, h) + OWN))
    for when, name in EXTRA:
        at(when, ("extra", name))
    free["z+"] = free["z-"] = 0.5
    for link, first in (("z+", 0), ("z-", 4)):
        for i in range(FIRST, 8):
            offer(link, 3 if i < 4 else 5, ("own", (first + i) % 8))
    for i in range(FIRST):
        at(HOP, ("relay", "z+", i))
        at(HOP, ("relay", "z-", 4 + i))
    while events:
        now, _, what = heapq.heappop(events)
        if what[0] == "take":
            steps.append(what)
            for link in routes(*what[1]):
                offer(link, rank(what[1], link), ("piece", what[1]))
        elif what[0] == "relay":
            offer(what[1], 4, ("relay", what[2]))
        elif what[0] == "extra":
            steps.append(what)
        for link in links:
            while waiting[link] and free[link] <= now + LEAD:
                _, _, (sort, which) = heapq.heappop(waiting[link])
                begin = max(free[link], now)
                free[link] = begin + PIECE * (1 if sort == "piece" else 2)
                steps.append((sort, which, link))
                landed = free[link] + HOP
                if sort == "piece":
                    at(landed, ("take", which[:2] + seen_from(link, *which[2:])))
                elif sort == "own" and (which < 4) == (link == "z+"):
                    at(landed, ("relay", link, which))
                at(free[link] - LEAD, ("turn",))
    return steps


def outer_step(master, moment, summed):
    difference = master - summed * 0.25
    velocity = 0.5 * moment + difference
    return master - 0.7 * (difference + 0.5 * velocity), velocity


def nt_dot(a, b):
    return lax.dot_general(a, b, (((1,), (1,)), ((), ())), preferred_element_type=F32)


SLOTS = {}


def slot(key):
    return SLOTS.setdefault(key, len(SLOTS))


N_RECV = 176
N_SEND = 72


def exchange(
    tu, td, te, tn, mu, vu, md, vd, me, ve, mn, vn, bt,
    RU, RD, RE, RN, SU, VU, SD, VD, SE, VE, SN, VN,
    tu_v, td_v, te_v, nb, mu_v, vu_v, md_v, vd_v, m_v, ve_v, mn_v, vn_v, bt_v,
    ru_a, ru_m, ru_p, rd_a, rd_m, rd_p, su, sd, cs, cr, xs, xr, so, tot,
    bs, mb, pf, pp, pr, wv, ms,
    lsem, ssem, gsem, rsem, csem,
):
    SLOTS.clear()
    z, s, t = lax.axis_index("replica"), lax.axis_index("shard"), lax.axis_index("tensor")
    y, x, c = lax.div(s, 4), lax.rem(lax.div(s, 2), 2), lax.rem(s, 2)
    zo = [z] + [lax.rem(z + i, 4) for i in (1, 2, 3)]
    yo = [y] + [lax.rem(y + i, 4) for i in (1, 2, 3)]
    xo = [x, 1 - x]
    devices = {
        "z+": (zo[1], s, t),
        "z-": (zo[3], s, t),
        "z2": (zo[2], s, t),
        "y+": (z, yo[1] * 4 + x * 2 + c, t),
        "y-": (z, yo[3] * 4 + x * 2 + c, t),
        "x": (z, y * 4 + xo[1] * 2 + c, t),
        "c": (z, y * 4 + x * 2 + (1 - c), t),
        "t": (z, s, 1 - t),
    }

    def block(o, p, e, core=c):
        return zo[o] * 16 + yo[p] * 4 + xo[e] * 2 + core

    loads = {}

    def load(name, src, dst):
        loads[name] = pltpu.make_async_copy(src, dst, lsem.at[len(loads)])
        loads[name].start()

    load("tu", tu.at[:, s], tu_v)
    load("td", td.at[:, s], td_v)
    load("mu", mu, mu_v)
    load("vu", vu, vu_v)
    load("md", md, md_v)
    load("vd", vd, vd_v)
    load("tn", tn, nb.at[z])
    load("me", me, m_v)
    load("bt", bt, bt_v)
    load("te", te, te_v)
    load("ve", ve, ve_v)
    load("mn", mn, mn_v)
    load("vn", vn, vn_v)

    barrier = pltpu.get_barrier_semaphore()
    for device in devices.values():
        pl.semaphore_signal(barrier, inc=1, device_id=device, device_id_type=MESH)
    pl.semaphore_wait(barrier, len(devices))

    single = []
    grouped = {}
    group_index = {"z+": 0, "z-": 1, "y+": 2, "y-": 3, "x": 4, "c": 5}

    def push(src, dst, key, direction):
        copy = pltpu.make_async_remote_copy(
            src, dst, ssem.at[len(single)], rsem.at[slot(key)], device_id=devices[direction], device_id_type=MESH
        )
        copy.start()
        single.append(copy)

    def arrived(ref, key):
        pltpu.make_async_remote_copy(
            ref, ref, ssem.at[0], rsem.at[slot(key)], device_id=devices["c"], device_id_type=MESH
        ).wait_recv()

    gathered = {"D": RD, "U": RU}
    half_rows = {"D": 16, "U": 8}

    def rows(kind, h):
        return pl.ds(h * half_rows[kind], half_rows[kind])

    def view(kind, h, o, p, e):
        return gathered[kind].at[block(o, p, e), rows(kind, h)]

    def forward(piece, direction):
        kind, h = piece[:2]
        ref = view(*piece)
        if direction == "c":
            recv = csem.at[0 if kind == "D" else 1]
        else:
            recv = rsem.at[slot((kind, h, seen_from(direction, *piece[2:])))]
        pltpu.make_async_remote_copy(
            ref, ref, gsem.at[group_index[direction]], recv, device_id=devices[direction], device_id_type=MESH
        ).start()
        grouped[direction] = grouped.get(direction, 0) + 1

    loads["tu"].wait()
    loads["td"].wait()
    for h in range(2):
        push(td_v.at[zo[2], rows("D", h)], rd_a.at[rows("D", h)], ("da", h), "z-")
        push(tu_v.at[zo[2], rows("U", h)], ru_a.at[rows("U", h)], ("ua", h), "z+")
    for h in range(2):
        push(td_v.at[zo[1], rows("D", h)], rd_m.at[rows("D", h)], ("dm", h), "z+")
        push(tu_v.at[zo[3], rows("U", h)], ru_p.at[rows("U", h)], ("up", h), "z-")

    on_low = t == 0

    def pick(low, high):
        return jnp.where(on_low, low, high)

    half = mu_v.shape[1] // 2
    loads["mu"].wait()
    loads["vu"].wait()
    m_other = pick(mu_v[:, half:], mu_v[:, :half])
    v_other = pick(vu_v[:, half:], vu_v[:, :half])
    cs[...] = (-0.05 * m_other - 0.175 * v_other).astype(BF16)
    push(cs, cr, "cr", "t")
    loads["tn"].wait()
    for direction, name in (("z+", "n3"), ("z-", "n1"), ("z2", "n2")):
        push(nb.at[z], nb.at[z], name, direction)

    loads["bt"].wait()
    high = bt_v[...].astype(BF16)
    bs[:64] = high
    bs[64:] = (bt_v[...] - high.astype(F32)).astype(BF16)
    loads["te"].wait()

    @pl.loop(0, 4)
    def _(j):
        both = nt_dot(bs[...], te_v[j])
        one = both[:64] + both[64:]
        pf[j] = one
        pp[j] = one.astype(BF16)

    for h in range(2):
        d, u = rows("D", h), rows("U", h)
        arrived(rd_a.at[d], ("da", h))
        sd[d] = (rd_a[d].astype(F32) + td_v[zo[3], d].astype(F32)).astype(BF16)
        push(sd.at[d], rd_p.at[d], ("dp", h), "z-")
        arrived(ru_a.at[u], ("ua", h))
        su[u] = (ru_a[u].astype(F32) + tu_v[zo[1], u].astype(F32)).astype(BF16)
        push(su.at[u], ru_m.at[u], ("um", h), "z+")

    loads["me"].wait()

    @pl.loop(0, 4)
    def _(k):
        mb[z * 4 + k] = m_v[k].astype(BF16)

    def master(o, j):
        return mb.at[zo[o] * 4 + j // 2, pl.ds(j % 2 * 32, 32)]

    def send_master(j, direction):
        push(master(0, j), master(0, j), ({"z+": "m-", "z-": "m+"}[direction], j), direction)

    def relay_master(j, direction):
        side, o = ("m-", 3) if direction == "z+" else ("m+", 1)
        arrived(master(o, j), (side, j))
        push(master(o, j), master(o, j), ("m2", j), direction)

    for i in range(FIRST):
        send_master(i, "z+")
        send_master(4 + i, "z-")
    for direction, o, name in (("z+", 1, "p3"), ("z-", 3, "p1"), ("z2", 2, "p2")):
        push(pp.at[zo[o]], pr.at[z], name, direction)

    loads["md"].wait()
    loads["vd"].wait()

    def own_down(h):
        d = rows("D", h)
        arrived(rd_m.at[d], ("dm", h))
        arrived(rd_p.at[d], ("dp", h))
        total = rd_p[d].astype(F32) + rd_m[d].astype(F32) + td_v[z, d].astype(F32)
        stored, velocity = outer_step(md_v[d], vd_v[d], total)
        RD[block(*OWN), d] = stored.astype(BF16)
        SD[d] = stored
        VD[d] = velocity

    def own_up(h):
        u = rows("U", h)
        arrived(ru_p.at[u], ("up", h))
        arrived(ru_m.at[u], ("um", h))
        if h == 0:
            arrived(cr, "cr")
        total = ru_m[u].astype(F32) + ru_p[u].astype(F32) + tu_v[z, u].astype(F32)
        m_own = pick(mu_v[:, :half], mu_v[:, half:])
        v_own = pick(vu_v[:, :half], vu_v[:, half:])
        mine = outer_step(m_own, v_own, total)[0]
        other = 0.2625 * total + cr[...].astype(F32)
        RU[block(*OWN), u] = jnp.where(t == h, mine, other).astype(BF16)
        tot[u] = total

    def swap():
        own, other = pick(tot[:8], tot[8:]), pick(tot[8:], tot[:8])
        so[...] = own
        xs[...] = other.astype(BF16)
        push(xs, xr, "xr", "t")

    def recast(o):
        w = wv[zo[o]].astype(F32).T

        for k in range(4):
            part = jnp.dot(w[k * 64 : (k + 1) * 64].astype(BF16), bs[:64], preferred_element_type=F32)
            if o == 0:
                new = m_v[k] - 0.7 * part
                SE[pl.ds(k * 64, 64)] = new
            else:
                new = mb[zo[o] * 4 + k].astype(F32) - 0.7 * part
            RE[zo[o] * 4 + k] = new.astype(BF16)

    def weights():
        loads["ve"].wait()
        for k in range(4):
            low = (m_v[k] - m_v[k].astype(BF16).astype(F32)).astype(BF16)
            both = nt_dot(bs[...], mb[z * 4 + k])
            ms[k] = both[:64] + both[64:] + nt_dot(bs[:64], low)
        for o in (1, 2, 3):
            arrived(pr.at[zo[o]], f"p{o}")
        total = pf[z] + pr[zo[1]].astype(F32) + pr[zo[2]].astype(F32) + pr[zo[3]].astype(F32)
        coefficient = jnp.concatenate([ms[k] for k in range(4)], axis=1) - 0.25 * total
        new = 0.5 * ve_v[...] + coefficient
        VE[...] = new
        wv[z] = (coefficient + 0.5 * new).astype(BF16)
        for direction, name in (("z+", "w3"), ("z-", "w1"), ("z2", "w2")):
            push(wv.at[z], wv.at[z], name, direction)
        recast(0)

    def local_steps():
        arrived(xr, "xr")
        for h in range(2):
            columns = pl.ds(h * half, half)
            mine = jnp.where(t == h, so[...], xr[...].astype(F32))
            stored, velocity = outer_step(mu_v[:, columns], vu_v[:, columns], mine)
            SU[:, columns] = stored
            VU[:, columns] = velocity
        for o in (1, 2, 3):
            arrived(nb.at[zo[o]], f"n{o}")
        loads["mn"].wait()
        loads["vn"].wait()
        total = nb[0].astype(F32) + nb[1].astype(F32) + nb[2].astype(F32) + nb[3].astype(F32)
        stored, velocity = outer_step(mn_v[...], vn_v[...], total)
        SN[...] = stored
        VN[...] = velocity
        RN[...] = stored.astype(BF16)

    def near_rows():
        for o, side in ((3, "m-"), (1, "m+")):
            for j in {"m-": (4, 5, 6, 7), "m+": (0, 1, 2, 3)}[side]:
                arrived(master(o, j), (side, j))
            arrived(wv.at[zo[o]], f"w{o}")
            recast(o)

    def far_rows():
        for j in range(8):
            arrived(master(2, j), ("m2", j))
        arrived(wv.at[zo[2]], "w2")
        recast(2)

    def take(kind, h, o, p, e):
        if (o, p, e) == OWN:
            {"D": own_down, "U": own_up}[kind](h)
        else:
            arrived(view(kind, h, o, p, e), (kind, h, (o, p, e)))
        forward((kind, h, o, p, e), "c")

    extra = {"weights": weights, "swap": swap, "local": local_steps, "near": near_rows, "far": far_rows}
    for step in plan():
        if step[0] == "take":
            take(*step[1])
        elif step[0] == "piece":
            forward(step[1], step[2])
        elif step[0] == "own":
            send_master(step[1], step[2])
        elif step[0] == "relay":
            relay_master(step[1], step[2])
        else:
            extra[step[1]]()

    for i, ref in enumerate((RD, RU)):
        landed = ref.at[pl.ds(0, 32)]
        pltpu.make_async_remote_copy(
            landed, landed, ssem.at[0], csem.at[i], device_id=devices["c"], device_id_type=MESH
        ).wait_recv()
    for copy in single:
        copy.wait_send()
    for direction, n in grouped.items():
        sent = RD.at[pl.ds(0, n // 2)] if n > 64 else RD.at[pl.ds(0, n), pl.ds(0, 16)]
        pltpu.make_async_remote_copy(
            sent, sent, gsem.at[group_index[direction]], rsem.at[0], device_id=devices["c"], device_id_type=MESH
        ).wait_send()


def flush(*refs):
    sources, targets, sem = refs[:12], refs[12:24], refs[24]
    copies = []
    for source, target in zip(sources, targets):
        pieces = 4 if source.shape[0] in (64, 16) and len(source.shape) == 3 else 1
        rows = source.shape[0] // pieces
        for i in range(pieces):
            part = pl.ds(i * rows, rows)
            copies.append(pltpu.make_async_copy(source.at[part], target.at[part], sem.at[len(copies)]))
            copies[-1].start()
    for copy in copies:
        copy.wait()


def body(
    trained_up,
    trained_down,
    trained_embed,
    trained_norm,
    master_up,
    moment_up,
    master_down,
    moment_down,
    master_embed,
    moment_embed,
    master_norm,
    moment_norm,
    embed_basis,
):
    operands = (
        trained_up.reshape(4, 16, 16, 2048),
        trained_down.reshape(4, 16, 32, 1024),
        trained_embed.reshape(4, 256, 1024),
        trained_norm[0],
        master_up,
        moment_up,
        master_down[0],
        moment_down[0],
        master_embed.reshape(4, 64, 1024),
        moment_embed[0].T,
        master_norm,
        moment_norm,
        embed_basis.T,
    )
    shapes = (
        ((64, 16, 2048), BF16),
        ((64, 32, 1024), BF16),
        ((16, 64, 1024), BF16),
        ((2, 1024), BF16),
        ((8, 4096), F32),
        ((8, 4096), F32),
        ((32, 1024), F32),
        ((32, 1024), F32),
        ((256, 1024), F32),
        ((64, 256), F32),
        ((2, 1024), F32),
        ((2, 1024), F32),
    )
    hbm = pl.BlockSpec(memory_space=pltpu.HBM)
    vmem = pl.BlockSpec(memory_space=pltpu.VMEM)
    new = pl.pallas_call(
        exchange,
        out_shape=tuple(pltpu.VMEM(shape, dtype) for shape, dtype in shapes),
        in_specs=[hbm] * 13,
        out_specs=[vmem] * 12,
        scratch_shapes=[
            pltpu.VMEM((4, 16, 2048), BF16),
            pltpu.VMEM((4, 32, 1024), BF16),
            pltpu.VMEM((4, 256, 1024), BF16),
            pltpu.VMEM((4, 2, 1024), BF16),
            pltpu.VMEM((8, 4096), F32),
            pltpu.VMEM((8, 4096), F32),
            pltpu.VMEM((32, 1024), F32),
            pltpu.VMEM((32, 1024), F32),
            pltpu.VMEM((4, 64, 1024), F32),
            pltpu.VMEM((64, 256), F32),
            pltpu.VMEM((2, 1024), F32),
            pltpu.VMEM((2, 1024), F32),
            pltpu.VMEM((64, 1024), F32),
            pltpu.VMEM((16, 2048), BF16),
            pltpu.VMEM((16, 2048), BF16),
            pltpu.VMEM((16, 2048), BF16),
            pltpu.VMEM((32, 1024), BF16),
            pltpu.VMEM((32, 1024), BF16),
            pltpu.VMEM((32, 1024), BF16),
            pltpu.VMEM((16, 2048), BF16),
            pltpu.VMEM((32, 1024), BF16),
            pltpu.VMEM((8, 2048), BF16),
            pltpu.VMEM((8, 2048), BF16),
            pltpu.VMEM((8, 2048), BF16),
            pltpu.VMEM((8, 2048), BF16),
            pltpu.VMEM((8, 2048), F32),
            pltpu.VMEM((16, 2048), F32),
            pltpu.VMEM((128, 1024), BF16),
            pltpu.VMEM((16, 64, 1024), BF16),
            pltpu.VMEM((4, 64, 256), F32),
            pltpu.VMEM((4, 64, 256), BF16),
            pltpu.VMEM((4, 64, 256), BF16),
            pltpu.VMEM((4, 64, 256), BF16),
            pltpu.VMEM((4, 64, 64), F32),
            pltpu.SemaphoreType.DMA((13,)),
            pltpu.SemaphoreType.DMA((N_SEND,)),
            pltpu.SemaphoreType.DMA((6,)),
            pltpu.SemaphoreType.DMA((N_RECV,)),
            pltpu.SemaphoreType.DMA((2,)),
        ],
        compiler_params=pltpu.CompilerParams(
            collective_id=0, has_side_effects=True, vmem_limit_bytes=24 << 20
        ),
        name="exchange",
    )(*[pltpu.with_memory_space_constraint(a, pltpu.HBM) for a in operands])
    new = [pltpu.with_memory_space_constraint(a, pltpu.VMEM) for a in new]
    out = pl.pallas_call(
        flush,
        out_shape=tuple(jax.ShapeDtypeStruct(shape, dtype) for shape, dtype in shapes),
        in_specs=[vmem] * 12,
        out_specs=[hbm] * 12,
        scratch_shapes=[pltpu.SemaphoreType.DMA((21,))],
        compiler_params=pltpu.CompilerParams(vmem_limit_bytes=1 << 20),
        name="flush",
    )(*new)
    return (
        out[0].reshape(1024, 2048),
        out[1].reshape(2048, 1024),
        out[2].reshape(1024, 1024),
        out[3],
        out[4],
        out[5],
        out[6][None],
        out[7][None],
        out[8][None],
        out[9].T[None],
        out[10],
        out[11],
    )


def solution(mesh):
    in_specs = (
        P("replica", None, "tensor"),
        P("replica", "tensor", None),
        P("replica", ("shard", "tensor"), None),
        P("replica", None, None),
        P(("replica", "shard", "tensor"), None),
        P(("replica", "shard", "tensor"), None),
        P("tensor", ("replica", "shard"), None),
        P("tensor", ("replica", "shard"), None),
        P(("shard", "tensor"), "replica", None),
        P(("shard", "tensor"), "replica", None),
        P(),
        P(),
        P(),
    )
    out_specs = (
        P(None, "tensor"),
        P("tensor", None),
        P(("shard", "tensor"), None),
        P(),
        P(("replica", "shard", "tensor"), None),
        P(("replica", "shard", "tensor"), None),
        P("tensor", ("replica", "shard"), None),
        P("tensor", ("replica", "shard"), None),
        P(("shard", "tensor"), "replica", None),
        P(("shard", "tensor"), "replica", None),
        P(),
        P(),
    )
    return jax.shard_map(body, mesh=mesh, in_specs=in_specs, out_specs=out_specs, check_vma=False)
```

```python
import heapq

import jax
import jax.numpy as jnp
from jax import lax
from jax.experimental import pallas as pl
from jax.experimental.pallas import tpu as pltpu
from jax.sharding import PartitionSpec as P

MESH = pl.DeviceIdType.MESH
F32, BF16 = jnp.float32, jnp.bfloat16

OWN = (0, 0, 0)


def routes(kind, h, o, p, e):
    z_part = {0: ["z+", "z-"], 3: ["z+"] * (h == 0), 1: ["z-"] * (h == 1), 2: []}[o]
    y_part = {0: ["y+", "y-"], 3: ["y+"] * (h == 0), 1: ["y-"] * (h == 1), 2: []}[p]
    if kind == "D":
        if e:
            return []
        return (z_part if p == 0 else []) + y_part + ["x"]
    if p:
        return y_part
    return (["x"] if o == 0 and e == 0 else []) + z_part + y_part


def seen_from(direction, o, p, e):
    if direction == "z+":
        return (o + 3) % 4, p, e
    if direction == "z-":
        return (o + 1) % 4, p, e
    if direction == "y+":
        return o, (p + 3) % 4, e
    if direction == "y-":
        return o, (p + 1) % 4, e
    return o, p, 1 - e


def rank(piece, direction):
    kind, h, o, p, e = piece
    if kind == "D":
        return 1 if direction == "x" else 0
    if direction[0] == "y":
        return 2 if p == 0 else 3
    return 0 if direction == "x" else 1


FIRST = 1
HOP, PIECE, LEAD = 2.0, 0.705, 2.1
READY = {("D", 0): 0.0, ("D", 1): 0.5, ("U", 0): 0.8, ("U", 1): 1.2}
EXTRA = [
    *((5.0 + j, "project", j) for j in range(4)),
    *((9.0 + 0.8 * k, "master", k) for k in range(4)),
    (12.2, "swap"),
    (13.0, "weights"),
    (14.0, "recast", 0, 0),
    (15.0, "recast", 0, 1),
    (17.0, "local"),
    (19.5, "recast", 2, 0),
    (20.5, "recast", 2, 1),
    (21.5, "recast", 3, 0),
    (22.5, "recast", 1, 1),
    (25.2, "recast", 3, 1),
    (25.4, "recast", 1, 0),
]


def plan():
    links = ["z+", "z-", "y+", "y-", "x"]
    free = dict.fromkeys(links, 0.0)
    waiting = {link: [] for link in links}
    events, steps = [], []

    def at(when, what):
        at.count += 1
        heapq.heappush(events, (when, at.count, what))

    def offer(link, order, what):
        at.count += 1
        heapq.heappush(waiting[link], (order, at.count, what))

    at.count = 0
    for (kind, h), when in READY.items():
        at(when, ("take", (kind, h) + OWN))
    for when, *call in EXTRA:
        at(when, ("extra", *call))
    free["z+"] = free["z-"] = 0.5
    for link, first in (("z+", 0), ("z-", 4)):
        for i in range(FIRST, 8):
            offer(link, 3 if i < 4 else 5, ("own", (first + i) % 8))
    for i in range(FIRST):
        at(HOP, ("relay", "z+", i))
        at(HOP, ("relay", "z-", 4 + i))
    while events:
        now, _, what = heapq.heappop(events)
        if what[0] == "take":
            steps.append(what)
            for link in routes(*what[1]):
                offer(link, rank(what[1], link), ("piece", what[1]))
        elif what[0] == "relay":
            offer(what[1], 4, ("relay", what[2]))
        elif what[0] == "extra":
            steps.append(what)
        for link in links:
            while waiting[link] and free[link] <= now + LEAD:
                _, _, (sort, which) = heapq.heappop(waiting[link])
                begin = max(free[link], now)
                free[link] = begin + PIECE * (1 if sort == "piece" else 2)
                steps.append((sort, which, link))
                landed = free[link] + HOP
                if sort == "piece":
                    at(landed, ("take", which[:2] + seen_from(link, *which[2:])))
                elif sort == "own" and (which < 4) == (link == "z+"):
                    at(landed, ("relay", link, which))
                at(free[link] - LEAD, ("turn",))
    return steps


def outer_step(master, moment, summed):
    difference = master - summed * 0.25
    velocity = 0.5 * moment + difference
    return master - 0.7 * (difference + 0.5 * velocity), velocity


def nt_dot(a, b):
    return lax.dot_general(a, b, (((1,), (1,)), ((), ())), preferred_element_type=F32)


SLOTS = {}


def slot(key):
    return SLOTS.setdefault(key, len(SLOTS))


N_RECV = 176
N_SEND = 72


def exchange(
    tu, td, te, tn, mu, vu, md, vd, me, ve, mn, vn, bt,
    RU, RD, RE, RN, SU, VU, SD, VD, SE, VE, SN, VN,
    tu_v, td_v, te_v, nb, mu_v, vu_v, md_v, vd_v, m_v, ve_v, mn_v, vn_v, bt_v,
    ru_a, ru_m, ru_p, rd_a, rd_m, rd_p, su, sd, cs, cr, xs, xr, so, tot,
    bs, mb, pf, pp, pr, wv, ms,
    lsem, ssem, gsem, rsem, csem,
):
    SLOTS.clear()
    z, s, t = lax.axis_index("replica"), lax.axis_index("shard"), lax.axis_index("tensor")
    y, x, c = lax.div(s, 4), lax.rem(lax.div(s, 2), 2), lax.rem(s, 2)
    zo = [z] + [lax.rem(z + i, 4) for i in (1, 2, 3)]
    yo = [y] + [lax.rem(y + i, 4) for i in (1, 2, 3)]
    xo = [x, 1 - x]
    devices = {
        "z+": (zo[1], s, t),
        "z-": (zo[3], s, t),
        "z2": (zo[2], s, t),
        "y+": (z, yo[1] * 4 + x * 2 + c, t),
        "y-": (z, yo[3] * 4 + x * 2 + c, t),
        "x": (z, y * 4 + xo[1] * 2 + c, t),
        "c": (z, y * 4 + x * 2 + (1 - c), t),
        "t": (z, s, 1 - t),
    }

    def block(o, p, e, core=c):
        return zo[o] * 16 + yo[p] * 4 + xo[e] * 2 + core

    loads = {}

    def load(name, src, dst):
        loads[name] = pltpu.make_async_copy(src, dst, lsem.at[len(loads)])
        loads[name].start()

    load("tu", tu.at[:, s], tu_v)
    load("td", td.at[:, s], td_v)
    load("mu", mu, mu_v)
    load("vu", vu, vu_v)
    load("md", md, md_v)
    load("vd", vd, vd_v)
    load("tn", tn, nb.at[z])
    load("me", me, m_v)
    load("bt", bt, bt_v)
    load("te", te, te_v)
    load("ve", ve, ve_v)
    load("mn", mn, mn_v)
    load("vn", vn, vn_v)

    barrier = pltpu.get_barrier_semaphore()
    for device in devices.values():
        pl.semaphore_signal(barrier, inc=1, device_id=device, device_id_type=MESH)
    pl.semaphore_wait(barrier, len(devices))

    single = []
    grouped = {}
    group_index = {"z+": 0, "z-": 1, "y+": 2, "y-": 3, "x": 4, "c": 5}

    def push(src, dst, key, direction):
        copy = pltpu.make_async_remote_copy(
            src, dst, ssem.at[len(single)], rsem.at[slot(key)], device_id=devices[direction], device_id_type=MESH
        )
        copy.start()
        single.append(copy)

    def arrived(ref, key):
        pltpu.make_async_remote_copy(
            ref, ref, ssem.at[0], rsem.at[slot(key)], device_id=devices["c"], device_id_type=MESH
        ).wait_recv()

    gathered = {"D": RD, "U": RU}
    half_rows = {"D": 16, "U": 8}

    def rows(kind, h):
        return pl.ds(h * half_rows[kind], half_rows[kind])

    def view(kind, h, o, p, e):
        return gathered[kind].at[block(o, p, e), rows(kind, h)]

    def forward(piece, direction):
        kind, h = piece[:2]
        ref = view(*piece)
        if direction == "c":
            recv = csem.at[0 if kind == "D" else 1]
        else:
            recv = rsem.at[slot((kind, h, seen_from(direction, *piece[2:])))]
        pltpu.make_async_remote_copy(
            ref, ref, gsem.at[group_index[direction]], recv, device_id=devices[direction], device_id_type=MESH
        ).start()
        grouped[direction] = grouped.get(direction, 0) + 1

    loads["tu"].wait()
    loads["td"].wait()
    for h in range(2):
        push(td_v.at[zo[2], rows("D", h)], rd_a.at[rows("D", h)], ("da", h), "z-")
        push(tu_v.at[zo[2], rows("U", h)], ru_a.at[rows("U", h)], ("ua", h), "z+")
    for h in range(2):
        push(td_v.at[zo[1], rows("D", h)], rd_m.at[rows("D", h)], ("dm", h), "z+")
        push(tu_v.at[zo[3], rows("U", h)], ru_p.at[rows("U", h)], ("up", h), "z-")

    on_low = t == 0

    def pick(low, high):
        return jnp.where(on_low, low, high)

    half = mu_v.shape[1] // 2
    loads["mu"].wait()
    loads["vu"].wait()
    m_other = pick(mu_v[:, half:], mu_v[:, :half])
    v_other = pick(vu_v[:, half:], vu_v[:, :half])
    cs[...] = (-0.05 * m_other - 0.175 * v_other).astype(BF16)
    push(cs, cr, "cr", "t")
    loads["tn"].wait()
    for direction, name in (("z+", "n3"), ("z-", "n1"), ("z2", "n2")):
        push(nb.at[z], nb.at[z], name, direction)

    for h in range(2):
        d, u = rows("D", h), rows("U", h)
        arrived(rd_a.at[d], ("da", h))
        sd[d] = (rd_a[d].astype(F32) + td_v[zo[3], d].astype(F32)).astype(BF16)
        push(sd.at[d], rd_p.at[d], ("dp", h), "z-")
        arrived(ru_a.at[u], ("ua", h))
        su[u] = (ru_a[u].astype(F32) + tu_v[zo[1], u].astype(F32)).astype(BF16)
        push(su.at[u], ru_m.at[u], ("um", h), "z+")

    loads["me"].wait()

    @pl.loop(0, 4)
    def _(k):
        mb[z * 4 + k] = m_v[k].astype(BF16)

    def master(o, j):
        return mb.at[zo[o] * 4 + j // 2, pl.ds(j % 2 * 32, 32)]

    def send_master(j, direction):
        push(master(0, j), master(0, j), ({"z+": "m-", "z-": "m+"}[direction], j), direction)

    def relay_master(j, direction):
        side, o = ("m-", 3) if direction == "z+" else ("m+", 1)
        arrived(master(o, j), (side, j))
        push(master(o, j), master(o, j), ("m2", j), direction)

    for i in range(FIRST):
        send_master(i, "z+")
        send_master(4 + i, "z-")
    loads["md"].wait()
    loads["vd"].wait()

    def own_down(h):
        d = rows("D", h)
        arrived(rd_m.at[d], ("dm", h))
        arrived(rd_p.at[d], ("dp", h))
        total = rd_p[d].astype(F32) + rd_m[d].astype(F32) + td_v[z, d].astype(F32)
        stored, velocity = outer_step(md_v[d], vd_v[d], total)
        RD[block(*OWN), d] = stored.astype(BF16)
        SD[d] = stored
        VD[d] = velocity

    def own_up(h):
        u = rows("U", h)
        arrived(ru_p.at[u], ("up", h))
        arrived(ru_m.at[u], ("um", h))
        if h == 0:
            arrived(cr, "cr")
        total = ru_m[u].astype(F32) + ru_p[u].astype(F32) + tu_v[z, u].astype(F32)
        m_own = pick(mu_v[:, :half], mu_v[:, half:])
        v_own = pick(vu_v[:, :half], vu_v[:, half:])
        mine = outer_step(m_own, v_own, total)[0]
        other = 0.2625 * total + cr[...].astype(F32)
        RU[block(*OWN), u] = jnp.where(t == h, mine, other).astype(BF16)
        tot[u] = total

    def swap():
        own, other = pick(tot[:8], tot[8:]), pick(tot[8:], tot[:8])
        so[...] = own
        xs[...] = other.astype(BF16)
        push(xs, xr, "xr", "t")

    def project(j):
        if j == 0:
            loads["bt"].wait()
            high = bt_v[...].astype(BF16)
            bs[:64] = high
            bs[64:] = (bt_v[...] - high.astype(F32)).astype(BF16)
            loads["te"].wait()
        both = nt_dot(bs[...], te_v[j])
        one = both[:64] + both[64:]
        pf[j] = one
        pp[j] = one.astype(BF16)
        if j == 3:
            for direction, o, name in (("z+", 1, "p3"), ("z-", 3, "p1"), ("z2", 2, "p2")):
                push(pp.at[zo[o]], pr.at[z], name, direction)

    def project_master(k):
        low = (m_v[k] - m_v[k].astype(BF16).astype(F32)).astype(BF16)
        both = nt_dot(bs[...], mb[z * 4 + k])
        ms[k] = both[:64] + both[64:] + nt_dot(bs[:64], low)

    def weights():
        loads["ve"].wait()
        for o in (1, 2, 3):
            arrived(pr.at[zo[o]], f"p{o}")
        total = pf[z] + pr[zo[1]].astype(F32) + pr[zo[2]].astype(F32) + pr[zo[3]].astype(F32)
        coefficient = jnp.concatenate([ms[k] for k in range(4)], axis=1) - 0.25 * total
        new = 0.5 * ve_v[...] + coefficient
        VE[...] = new
        wv[z] = (coefficient + 0.5 * new).astype(BF16)
        for direction, name in (("z+", "w3"), ("z-", "w1"), ("z2", "w2")):
            push(wv.at[z], wv.at[z], name, direction)

    seen = set()

    def recast(o, q):
        if o and o not in seen:
            seen.add(o)
            arrived(wv.at[zo[o]], f"w{o}")
        for j in range(4 * q, 4 * q + 4):
            if o == 2:
                arrived(master(2, j), ("m2", j))
            elif o == 3 and q == 1:
                arrived(master(3, j), ("m-", j))
            elif o == 1 and q == 0:
                arrived(master(1, j), ("m+", j))
        w = wv[zo[o], :, q * 128 : (q + 1) * 128].astype(F32).T
        for i in range(2):
            k = 2 * q + i
            part = jnp.dot(w[i * 64 : (i + 1) * 64].astype(BF16), bs[:64], preferred_element_type=F32)
            if o == 0:
                new = m_v[k] - 0.7 * part
                SE[pl.ds(k * 64, 64)] = new
            else:
                new = mb[zo[o] * 4 + k].astype(F32) - 0.7 * part
            RE[zo[o] * 4 + k] = new.astype(BF16)

    def local_steps():
        arrived(xr, "xr")
        for h in range(2):
            columns = pl.ds(h * half, half)
            mine = jnp.where(t == h, so[...], xr[...].astype(F32))
            stored, velocity = outer_step(mu_v[:, columns], vu_v[:, columns], mine)
            SU[:, columns] = stored
            VU[:, columns] = velocity
        for o in (1, 2, 3):
            arrived(nb.at[zo[o]], f"n{o}")
        loads["mn"].wait()
        loads["vn"].wait()
        total = nb[0].astype(F32) + nb[1].astype(F32) + nb[2].astype(F32) + nb[3].astype(F32)
        stored, velocity = outer_step(mn_v[...], vn_v[...], total)
        SN[...] = stored
        VN[...] = velocity
        RN[...] = stored.astype(BF16)

    def take(kind, h, o, p, e):
        if (o, p, e) == OWN:
            {"D": own_down, "U": own_up}[kind](h)
        else:
            arrived(view(kind, h, o, p, e), (kind, h, (o, p, e)))
        forward((kind, h, o, p, e), "c")

    extra = {
        "project": project,
        "master": project_master,
        "weights": weights,
        "swap": swap,
        "local": local_steps,
        "recast": recast,
    }
    for step in plan():
        if step[0] == "take":
            take(*step[1])
        elif step[0] == "piece":
            forward(step[1], step[2])
        elif step[0] == "own":
            send_master(step[1], step[2])
        elif step[0] == "relay":
            relay_master(step[1], step[2])
        else:
            extra[step[1]](*step[2:])

    for i, ref in enumerate((RD, RU)):
        landed = ref.at[pl.ds(0, 32)]
        pltpu.make_async_remote_copy(
            landed, landed, ssem.at[0], csem.at[i], device_id=devices["c"], device_id_type=MESH
        ).wait_recv()
    for copy in single:
        copy.wait_send()
    for direction, n in grouped.items():
        sent = RD.at[pl.ds(0, n // 2)] if n > 64 else RD.at[pl.ds(0, n), pl.ds(0, 16)]
        pltpu.make_async_remote_copy(
            sent, sent, gsem.at[group_index[direction]], rsem.at[0], device_id=devices["c"], device_id_type=MESH
        ).wait_send()


def flush(*refs):
    sources, targets, sem = refs[:12], refs[12:24], refs[24]
    copies = []
    for source, target in zip(sources, targets):
        pieces = 4 if source.shape[0] in (64, 16) and len(source.shape) == 3 else 1
        rows = source.shape[0] // pieces
        for i in range(pieces):
            part = pl.ds(i * rows, rows)
            copies.append(pltpu.make_async_copy(source.at[part], target.at[part], sem.at[len(copies)]))
            copies[-1].start()
    for copy in copies:
        copy.wait()


def body(
    trained_up,
    trained_down,
    trained_embed,
    trained_norm,
    master_up,
    moment_up,
    master_down,
    moment_down,
    master_embed,
    moment_embed,
    master_norm,
    moment_norm,
    embed_basis,
):
    operands = (
        trained_up.reshape(4, 16, 16, 2048),
        trained_down.reshape(4, 16, 32, 1024),
        trained_embed.reshape(4, 256, 1024),
        trained_norm[0],
        master_up,
        moment_up,
        master_down[0],
        moment_down[0],
        master_embed.reshape(4, 64, 1024),
        moment_embed[0].T,
        master_norm,
        moment_norm,
        embed_basis.T,
    )
    shapes = (
        ((64, 16, 2048), BF16),
        ((64, 32, 1024), BF16),
        ((16, 64, 1024), BF16),
        ((2, 1024), BF16),
        ((8, 4096), F32),
        ((8, 4096), F32),
        ((32, 1024), F32),
        ((32, 1024), F32),
        ((256, 1024), F32),
        ((64, 256), F32),
        ((2, 1024), F32),
        ((2, 1024), F32),
    )
    hbm = pl.BlockSpec(memory_space=pltpu.HBM)
    vmem = pl.BlockSpec(memory_space=pltpu.VMEM)
    new = pl.pallas_call(
        exchange,
        out_shape=tuple(pltpu.VMEM(shape, dtype) for shape, dtype in shapes),
        in_specs=[hbm] * 13,
        out_specs=[vmem] * 12,
        scratch_shapes=[
            pltpu.VMEM((4, 16, 2048), BF16),
            pltpu.VMEM((4, 32, 1024), BF16),
            pltpu.VMEM((4, 256, 1024), BF16),
            pltpu.VMEM((4, 2, 1024), BF16),
            pltpu.VMEM((8, 4096), F32),
            pltpu.VMEM((8, 4096), F32),
            pltpu.VMEM((32, 1024), F32),
            pltpu.VMEM((32, 1024), F32),
            pltpu.VMEM((4, 64, 1024), F32),
            pltpu.VMEM((64, 256), F32),
            pltpu.VMEM((2, 1024), F32),
            pltpu.VMEM((2, 1024), F32),
            pltpu.VMEM((64, 1024), F32),
            pltpu.VMEM((16, 2048), BF16),
            pltpu.VMEM((16, 2048), BF16),
            pltpu.VMEM((16, 2048), BF16),
            pltpu.VMEM((32, 1024), BF16),
            pltpu.VMEM((32, 1024), BF16),
            pltpu.VMEM((32, 1024), BF16),
            pltpu.VMEM((16, 2048), BF16),
            pltpu.VMEM((32, 1024), BF16),
            pltpu.VMEM((8, 2048), BF16),
            pltpu.VMEM((8, 2048), BF16),
            pltpu.VMEM((8, 2048), BF16),
            pltpu.VMEM((8, 2048), BF16),
            pltpu.VMEM((8, 2048), F32),
            pltpu.VMEM((16, 2048), F32),
            pltpu.VMEM((128, 1024), BF16),
            pltpu.VMEM((16, 64, 1024), BF16),
            pltpu.VMEM((4, 64, 256), F32),
            pltpu.VMEM((4, 64, 256), BF16),
            pltpu.VMEM((4, 64, 256), BF16),
            pltpu.VMEM((4, 64, 256), BF16),
            pltpu.VMEM((4, 64, 64), F32),
            pltpu.SemaphoreType.DMA((13,)),
            pltpu.SemaphoreType.DMA((N_SEND,)),
            pltpu.SemaphoreType.DMA((6,)),
            pltpu.SemaphoreType.DMA((N_RECV,)),
            pltpu.SemaphoreType.DMA((2,)),
        ],
        compiler_params=pltpu.CompilerParams(
            collective_id=0, has_side_effects=True, vmem_limit_bytes=24 << 20
        ),
        name="exchange",
    )(*[pltpu.with_memory_space_constraint(a, pltpu.HBM) for a in operands])
    new = [pltpu.with_memory_space_constraint(a, pltpu.VMEM) for a in new]
    out = pl.pallas_call(
        flush,
        out_shape=tuple(jax.ShapeDtypeStruct(shape, dtype) for shape, dtype in shapes),
        in_specs=[vmem] * 12,
        out_specs=[hbm] * 12,
        scratch_shapes=[pltpu.SemaphoreType.DMA((21,))],
        compiler_params=pltpu.CompilerParams(vmem_limit_bytes=1 << 20),
        name="flush",
    )(*new)
    return (
        out[0].reshape(1024, 2048),
        out[1].reshape(2048, 1024),
        out[2].reshape(1024, 1024),
        out[3],
        out[4],
        out[5],
        out[6][None],
        out[7][None],
        out[8][None],
        out[9].T[None],
        out[10],
        out[11],
    )


def solution(mesh):
    in_specs = (
        P("replica", None, "tensor"),
        P("replica", "tensor", None),
        P("replica", ("shard", "tensor"), None),
        P("replica", None, None),
        P(("replica", "shard", "tensor"), None),
        P(("replica", "shard", "tensor"), None),
        P("tensor", ("replica", "shard"), None),
        P("tensor", ("replica", "shard"), None),
        P(("shard", "tensor"), "replica", None),
        P(("shard", "tensor"), "replica", None),
        P(),
        P(),
        P(),
    )
    out_specs = (
        P(None, "tensor"),
        P("tensor", None),
        P(("shard", "tensor"), None),
        P(),
        P(("replica", "shard", "tensor"), None),
        P(("replica", "shard", "tensor"), None),
        P("tensor", ("replica", "shard"), None),
        P("tensor", ("replica", "shard"), None),
        P(("shard", "tensor"), "replica", None),
        P(("shard", "tensor"), "replica", None),
        P(),
        P(),
    )
    return jax.shard_map(body, mesh=mesh, in_specs=in_specs, out_specs=out_specs, check_vma=False)
```
